32 devices in a mesh: branch: 2 (over z_hi), seq: 2 (over z_lo), dp: 8 (over y, x, core).
Axes of the slice: x: 2, y: 2, z: 4 (z_hi: 2, z_lo: 2; z = z_hi * 2 + z_lo), core: 2. Of those that a mesh axis runs over, the one named last changes fastest.
Arguments:
- qkv: bfloat16 [8, 224, 3, 3072], P('dp', 'seq'), may hold values from -14 to 14
- hidden: bfloat16 [8, 224, 5120], P('dp'), may hold values from -6 to 6
- weight: bfloat16 [5120, 3072], P('dp', ('branch', 'seq')), may hold values from -0.078125 to 0.078125
- lengths: int32 [8], replicated, may hold values from 112 to 224, as said below
- timestep_ids: int32 [8], replicated, may hold values from 0 to 999
- guide_scale: float32 [1000], replicated, may hold values from 1 to 3
Outputs:
- gradient: float32 [5120, 3072], P('dp', ('branch', 'seq'))
The draws below stay inside these ranges and needn't reach their ends.
Inputs may be any that keep to these rules, and one draw needn't show every extreme that they name: `lengths`: each sample has at least 112 valid tokens, and some sample has all 224.
All inputs are finite; a program needn't handle non-finite values.
Results may differ from the reference program's by a relative error of at most 0.0028.
Values may be sent and summed in bfloat16 or wider, within the bound.
A program may use at most 128 MiB of HBM per device.

```python
import math
import jax
import jax.numpy as jnp
from jax import lax

D = 5120
HEAD_DIM = 128
HEADS = 24
TSTEPS = 1000
L = 224
SAMPLES = 8
HD = 3072


def draw_qkv(key, part):
    base = jnp.clip(jax.random.normal(key, (SAMPLES, L, 3, HD), jnp.float32), -4.0, 4.0)
    return base.astype(jnp.bfloat16)


def draw_lengths(key, part):
    first_key, second_key = jax.random.split(jax.random.fold_in(key, 5))
    drawn = jax.random.randint(first_key, (SAMPLES,), L // 2, L + 1)
    chosen = jax.random.randint(second_key, (), 0, SAMPLES)
    return jnp.where(jnp.arange(SAMPLES) == chosen, L, drawn).astype(jnp.int32)


def touch_ends(values, rng, low, high):
    place = [jax.random.randint(jax.random.fold_in(rng, axis), (), 0, length) for axis, length in enumerate(values.shape)]
    widest = values.shape.index(max(values.shape))
    neighbour = place[:widest] + [(place[widest] + 1) % values.shape[widest]] + place[widest + 1:]
    return values.at[tuple(place)].set(low).at[tuple(neighbour)].set(high)


def raised(values, key, source, target, blocks, factor):
    owner, partner = [(jnp.arange(values.shape[dim]) // (values.shape[dim] // blocks)).reshape([-1 if axis == dim else 1 for axis in range(values.ndim)]) for dim in (source, target)]
    chosen = jax.random.permutation(key, blocks)[partner]
    strong = (owner == chosen) | (owner == (partner + blocks // 2) % blocks)
    return jnp.where(strong, factor * values, values)


def block_levels(rng, dims, shards, low, largest):
    gain, own = 1.0, jax.random.fold_in(rng, 6)
    for dim, shards_of in shards:
        steps = jnp.exp(jax.random.uniform(jax.random.fold_in(own, dim), (shards_of,), jnp.float32, low / len(shards), largest / len(shards)))
        gain = gain * jnp.repeat(steps, dims[dim] // shards_of).reshape([-1 if axis == dim else 1 for axis in range(len(dims))])
    return gain


def noise(rng, shape, deviation, limit, cuts=(), held_as=jnp.bfloat16):
    factor_of = block_levels(rng, shape, cuts, -0.22, 0.18) if cuts else 1.0
    values = jax.random.normal(rng, shape, jnp.float32) * deviation * factor_of
    return jnp.minimum(jnp.maximum(values, -limit), limit).astype(held_as)


def heavy_noise(key, extent, scale, reach, cuts, heavy, kind=jnp.bfloat16):
    values = scale * jax.random.normal(key, extent, jnp.float32)
    if cuts:
        values = values * block_levels(key, extent, cuts, -0.22, 0.18)
    return jnp.clip(raised(values, jax.random.fold_in(key, 3), *heavy), -reach, reach).astype(kind)


def setup_inputs(seed: int = 0) -> dict:
    streams_of = jax.random.split(jax.random.key(seed), 7)
    qkv = draw_qkv(jax.random.fold_in(streams_of[6], 71), 0)
    hidden = heavy_noise(streams_of[1], (SAMPLES, L, D), 1.0, 6.0, ((0, 8),), (0, 2, 8, 2.0))
    weight = noise(streams_of[2], (D, HD), D ** -0.5, 0.078125, ((0, 8), (1, 4)))
    lengths = draw_lengths(jax.random.fold_in(streams_of[6], 71), 0)
    timestep_ids = touch_ends(jax.random.randint(streams_of[4], (SAMPLES,), 0, TSTEPS), jax.random.fold_in(streams_of[4], 1), 0, TSTEPS - 1).astype(jnp.int32)
    guide_scale = jnp.clip(jnp.exp(jax.random.uniform(streams_of[5], (TSTEPS,), jnp.float32, math.log(1.0), math.log(3.0))), 1.0, 3.0)
    return dict(qkv=qkv, hidden=hidden, weight=weight, lengths=lengths, timestep_ids=timestep_ids, guide_scale=guide_scale)


def attend(sample_qkv, length):
    queries = sample_qkv[:, 0, :].reshape(L, HEADS, HEAD_DIM).astype(jnp.float32)
    keys_all = sample_qkv[:, 1, :].reshape(L, HEADS, HEAD_DIM).astype(jnp.float32)
    values = sample_qkv[:, 2, :].reshape(L, HEADS, HEAD_DIM).astype(jnp.float32)
    scores = jnp.einsum('qhd,khd->hqk', queries, keys_all) / math.sqrt(HEAD_DIM)
    key_valid = jnp.arange(L, dtype=jnp.int32) < length
    scores = jnp.where(key_valid[None, None, :], scores, -jnp.inf)
    maximum = lax.optimization_barrier(jnp.max(scores, axis=-1, keepdims=True))
    expo = jnp.exp(scores - maximum)
    probs = (expo / lax.optimization_barrier(jnp.sum(expo, axis=-1, keepdims=True))).astype(jnp.bfloat16)
    output = jnp.einsum('hqk,khd->qhd', probs.astype(jnp.float32), values)
    return output.astype(jnp.bfloat16).reshape(L, HD)

def reference(qkv, hidden, weight, lengths, timestep_ids, guide_scale):
    positions = jnp.arange(L, dtype=jnp.int32)

    def one_sample(totals, sample_items):
        sample_qkv, rows_h, length, step_id = sample_items
        guidance = jnp.sum(jnp.where(jnp.arange(TSTEPS, dtype=jnp.int32) == step_id, guide_scale, jnp.float32(0.0)))
        strong = attend(sample_qkv, length).astype(jnp.float32)
        weak_out = sample_qkv[:, 2, :].astype(jnp.float32)
        target = strong + guidance * (strong - weak_out)
        predicted = jnp.dot(rows_h, weight, preferred_element_type=jnp.float32)
        valid_rows = (positions < length)[:, None]
        scaled = (jnp.where(valid_rows, predicted - target, jnp.float32(0.0)) / SAMPLES).astype(jnp.bfloat16)
        return (totals + jnp.dot(rows_h.T, scaled, preferred_element_type=jnp.float32), None)
    totals, _ = lax.scan(one_sample, jnp.zeros((D, HD), jnp.float32), (qkv, hidden, lengths, timestep_ids))
    return totals
```

```python
import functools
import math

import jax
import jax.numpy as jnp
from jax import lax
from jax.experimental import pallas as pl
from jax.experimental.pallas import tpu as pltpu
from jax.sharding import PartitionSpec as P

HEAD_DIM = 128
MESH = pl.DeviceIdType.MESH
VMEM_BYTES = 58500000


def flip(index, bits, count):
    out, step = 0, 1
    while step < count:
        bit = lax.rem(index // step, 2)
        out = out + (lax.rem(bit + 1, 2) if bits & step else bit) * step
        step *= 2
    return out


def kernel(
    n, share,
    lengths_ref, steps_ref, guide_ref, qkv_ref, hidden_ref, weight_ref, out_ref,
    qbuf, hbuf, hx, wbuf, tgt, pf, pbuf, pown, prec, rbuf, dbuf, dsib,
    loc, h_s, h_r, z_s, z_r, w_s, w_r, q_s, q_r, f_s, f_r, p_s, p_r, d_s, d_r, x_s, x_r, r_s, r_r, g_s, g_r,
):
    groups = n // 2
    me = lax.axis_index("dp")
    branch, seq = lax.axis_index("branch"), lax.axis_index("seq")
    core = lax.rem(me, 2)
    group = me // 2
    sib = {"dp": group * 2 + (1 - core)}
    pair = {"seq": 1 - seq}
    part = qkv_ref.shape[1]
    tokens = hidden_ref.shape[1]
    rows, cols = weight_ref.shape
    other_groups = [flip(group, r, groups) for r in range(groups)]
    peers = [{"dp": g * 2 + core} for g in other_groups]
    direct = tokens - 2 * share
    chunks = [
        (0, share, pl.multiple_of(seq * share, 16)),
        (share, direct, 2 * share),
        (share + direct, share, pl.multiple_of((1 - seq) * share, 16)),
    ]
    order = list(range(groups - 1, 0, -1))

    def remote(src, dst, send, recv, where):
        return pltpu.make_async_remote_copy(
            src_ref=src, dst_ref=dst, send_sem=send, recv_sem=recv,
            device_id=where, device_id_type=MESH,
        )

    def hid(g, chunk, start, width):
        base = pl.multiple_of(g * (2 * rows) + start, 128)
        return hidden_ref.at[0, pl.ds(chunk[2], chunk[1]), pl.ds(base, width)]

    def heads_of(to):
        return qkv_ref.at[:, :, pl.ds(pl.multiple_of((branch * 2 + to) * cols, 128), cols)]

    def at_rows(chunk):
        return pl.ds(chunk[0], chunk[1])

    barrier = pltpu.get_barrier_semaphore()
    for where in peers[1:] + [sib, pair]:
        pl.semaphore_signal(barrier, inc=1, device_id=where, device_id_type=MESH)
    my_rows = pl.ds(pl.multiple_of(core * rows, 128), rows)
    my_part = pl.ds(pl.multiple_of(seq * part, 16), part)
    local = [
        pltpu.make_async_copy(hid(group, chunk, 0, 2 * rows), hbuf.at[0, at_rows(chunk)], loc.at[c])
        for c, chunk in enumerate(chunks)
    ]
    local.append(pltpu.make_async_copy(weight_ref, wbuf.at[my_rows], loc.at[3]))
    local_q = pltpu.make_async_copy(
        heads_of(seq),
        qbuf.at[:, my_part], loc.at[4],
    )
    for copy in local + [local_q]:
        copy.start()
    pl.semaphore_wait(barrier, groups + 1)

    sent = []
    h_copies = {}
    for c in (0, 1):
        for r in order:
            h_copies[r, c] = remote(
                hid(other_groups[r], chunks[c], 0, 2 * rows), hbuf.at[r, at_rows(chunks[c])],
                h_s.at[r, c], h_r.at[r, c], peers[r],
            )
            h_copies[r, c].start()
            sent.append(h_copies[r, c])
    w_copy = remote(weight_ref, wbuf.at[my_rows], w_s.at[0], w_r.at[0], sib)
    w_copy.start()
    q_copy = remote(
        heads_of(1 - seq),
        qbuf.at[:, my_part], q_s.at[0], q_r.at[0], pair,
    )
    q_copy.start()
    sib_start = (1 - core) * rows
    sib_cols = pl.ds(pl.multiple_of(sib_start, 128), rows)
    f_copies = {}
    for c in range(3):
        f_copies[0, c] = remote(
            hid(group, chunks[c], sib_start, rows), hx.at[0, at_rows(chunks[c])],
            f_s.at[0, c], f_r.at[0, c], sib,
        )
        f_copies[0, c].start()
    sent += [w_copy, q_copy]

    length = lengths_ref[me]
    guidance = guide_ref[steps_ref[me]]

    step = 256 if cols % 256 == 0 else 128
    for copy in local:
        copy.wait()
    w_copy.wait_recv()

    @pl.loop(0, cols // step)
    def _(i):
        at = pl.ds(pl.multiple_of(i * step, 128), step)
        pown[:, at] = jnp.dot(hbuf[0], wbuf[:, at], preferred_element_type=jnp.float32)

    z_copies = {}
    p_copies = {}
    g_copies = {}
    halves = [None, slice(0, cols // 2), slice(cols // 2, cols)]

    def predict(c):
        chunk = chunks[c]
        first, count, _ = chunk
        for r in order:
            if c == 2:
                z_copies[r].wait_recv()
            else:
                h_copies[r, c].wait_recv()
            if c == 0:
                z_copies[r] = remote(
                    hbuf.at[r, at_rows(chunks[0])], hbuf.at[r, at_rows(chunks[2])],
                    z_s.at[r], z_r.at[r], pair,
                )
                z_copies[r].start()
                sent.append(z_copies[r])
            f_copies[r, c] = remote(
                hbuf.at[r, at_rows(chunk), sib_cols], hx.at[r, at_rows(chunk)],
                f_s.at[r, c], f_r.at[r, c], sib,
            )
            f_copies[r, c].start()

        @pl.loop(0, cols // step)
        def _(i):
            at = pl.ds(pl.multiple_of(i * step, 128), step)
            left = hbuf[1:, first:first + count, :].reshape((groups - 1) * count, 2 * rows)
            value = jnp.dot(left, wbuf[:, at], preferred_element_type=jnp.float32)
            pf[:, first:first + count, at] = value.reshape(groups - 1, count, step)

        for r in (1, 2):
            pbuf[3, first:first + count, halves[r]] = pf[2, first:first + count, halves[r]].astype(
                jnp.bfloat16
            )
            g_copies[r, c] = remote(
                pbuf.at[3, at_rows(chunk), halves[r]], rbuf.at[r - 1, at_rows(chunk)],
                g_s.at[r, c], g_r.at[r, c], peers[r],
            )
            g_copies[r, c].start()
            sent.append(g_copies[r, c])
        for r in (1, 2):
            pbuf[r, first:first + count, halves[r]] = pf[
                r - 1, first:first + count, halves[r]
            ].astype(jnp.bfloat16)
            send_term(r, c, halves[r], 0)

    def send_term(r, c, at, stage):
        slot = r + 2 * stage - 1
        p_copies[r, c, stage] = remote(
            pbuf.at[r, at_rows(chunks[c]), at], prec.at[r - 1, at_rows(chunks[c]), at],
            p_s.at[slot, c], p_r.at[slot, c], peers[r],
        )
        p_copies[r, c, stage].start()
        sent.append(p_copies[r, c, stage])

    def combine(c):
        first, count, _ = chunks[c]
        for r in (1, 2):
            g_copies[r, c].wait_recv()
            to, at = 3 - r, halves[r]
            value = pf[to - 1, first:first + count, at] + rbuf[
                r - 1, first:first + count, :
            ].astype(jnp.float32)
            pbuf[to, first:first + count, at] = value.astype(jnp.bfloat16)
            send_term(to, c, at, 1)

    d_copies = {}
    r_copies = {}
    x_copies = {}

    def to_sib(r, c):
        x_copies[r, c] = remote(
            dbuf.at[r, at_rows(chunks[c])], dsib.at[r, at_rows(chunks[c])],
            x_s.at[r, c], x_r.at[r, c], sib,
        )
        x_copies[r, c].start()

    def difference(c):
        first, count, token = chunks[c]
        total = pown[first:first + count, :] - tgt[pl.ds(token, count), :]
        for r in (1, 2):
            for stage in (0, 1):
                p_copies[r, c, stage].wait_recv()
            total = total + prec[r - 1, first:first + count, :].astype(jnp.float32)
        valid = token + lax.broadcasted_iota(jnp.int32, total.shape, 0) < length
        delta = jnp.where(valid, total, jnp.float32(0.0)) * jnp.float32(1.0 / n)
        dbuf[0, first:first + count, :] = delta.astype(jnp.bfloat16)
        for r in (1, 2):
            d_copies[r, c] = remote(
                dbuf.at[0, at_rows(chunks[c])], dbuf.at[r, at_rows(chunks[c])],
                d_s.at[r, c], d_r.at[r, c], peers[r],
            )
            d_copies[r, c].start()
            sent.append(d_copies[r, c])
        to_sib(0, c)

    def relay(c):
        for r in (1, 2):
            d_copies[r, c].wait_recv()
            at = pl.ds((r - 1) * (cols // 2), cols // 2)
            r_copies[r, c] = remote(
                dbuf.at[r, at_rows(chunks[c]), at], dbuf.at[3, at_rows(chunks[c]), at],
                r_s.at[r, c], r_r.at[r, c], peers[3 - r],
            )
            r_copies[r, c].start()
            sent.append(r_copies[r, c])
            to_sib(r, c)

    def finish(c):
        for r in (1, 2):
            r_copies[r, c].wait_recv()
        to_sib(3, c)

    predict(0)

    local_q.wait()
    q_copy.wait_recv()
    key_valid = lax.broadcasted_iota(jnp.int32, (tokens, tokens), 1) < length

    @pl.loop(0, cols // HEAD_DIM)
    def _(h):
        at = pl.ds(pl.multiple_of(h * HEAD_DIM, HEAD_DIM), HEAD_DIM)
        q, k, v = qbuf[0, :, at], qbuf[1, :, at], qbuf[2, :, at]
        scores = lax.dot_general(
            q, k, (((1,), (1,)), ((), ())), preferred_element_type=jnp.float32
        ) * jnp.float32(1.0 / math.sqrt(HEAD_DIM))
        scores = jnp.where(key_valid, scores, -jnp.inf)
        maximum = jnp.max(scores, axis=-1, keepdims=True)
        expo = jnp.exp(scores - maximum)
        probs = (expo / jnp.sum(expo, axis=-1, keepdims=True)).astype(jnp.bfloat16)
        strong = jnp.dot(probs, v, preferred_element_type=jnp.float32)
        strong = strong.astype(jnp.bfloat16).astype(jnp.float32)
        tgt[:, at] = strong + guidance * (strong - v.astype(jnp.float32))

    combine(0)
    predict(1)
    difference(0)
    combine(1)
    predict(2)
    relay(0)
    difference(1)
    combine(2)
    difference(2)
    relay(1)
    finish(0)
    finish(1)

    tile = 128

    def add(h_ref, base, d_ref, first, count, fresh=False):
        depth = groups * count

        @pl.loop(0, rows // tile)
        def _(i):
            start = pl.multiple_of(base + i * tile, tile)
            left = h_ref[:, first:first + count, pl.ds(start, tile)].reshape(depth, tile)
            right = d_ref[:, first:first + count, :].reshape(depth, cols)
            value = lax.dot_general(
                left, right, (((0,), (0,)), ((), ())), preferred_element_type=jnp.float32
            )
            at = pl.ds(pl.multiple_of(i * tile, tile), tile)
            if fresh:
                out_ref[at, :] = value
            else:
                out_ref[at, :] += value

    early, late = share + direct, share
    relay(2)
    add(hbuf, core * rows, dbuf, 0, early, fresh=True)
    for r in range(groups):
        for c in range(3):
            f_copies[r, c].wait_recv()
        for c in (0, 1):
            x_copies[r, c].wait_recv()
    add(hx, 0, dsib, 0, early)
    finish(2)
    add(hbuf, core * rows, dbuf, early, late)
    for r in range(groups):
        x_copies[r, 2].wait_recv()
    add(hx, 0, dsib, early, late)

    for copy in sent + list(f_copies.values()) + list(x_copies.values()):
        copy.wait_send()


def fused(n, seqs, qkv, hidden, weight, lengths, timestep_ids, guide_scale):
    part = qkv.shape[1]
    tokens, width = hidden.shape[1], hidden.shape[2]
    rows, cols = weight.shape
    groups = n // 2
    share = tokens * 5 // 14 // 16 * 16
    here = jnp.transpose(qkv[0], (1, 0, 2))
    dma = pltpu.SemaphoreType.DMA
    bf16, f32 = jnp.bfloat16, jnp.float32
    smem = pl.BlockSpec(memory_space=pltpu.SMEM)
    anywhere = pl.BlockSpec(memory_space=pltpu.HBM)
    return pl.pallas_call(
        functools.partial(kernel, n, share),
        out_shape=pltpu.VMEM((rows, cols), f32),
        in_specs=[smem, smem, smem, anywhere, anywhere, anywhere],
        out_specs=pl.BlockSpec(memory_space=pltpu.VMEM),
        scratch_shapes=[
            pltpu.VMEM((3, tokens, cols), bf16),
            pltpu.VMEM((groups, tokens, 2 * rows), bf16),
            pltpu.VMEM((groups, tokens, rows), bf16),
            pltpu.VMEM((2 * rows, cols), bf16),
            pltpu.VMEM((tokens, cols), f32),
            pltpu.VMEM((groups - 1, tokens, cols), f32),
            pltpu.VMEM((groups, tokens, cols), bf16),
            pltpu.VMEM((tokens, cols), f32),
            pltpu.VMEM((2, tokens, cols), bf16),
            pltpu.VMEM((2, tokens, cols // 2), bf16),
            pltpu.VMEM((groups, tokens, cols), bf16),
            pltpu.VMEM((groups, tokens, cols), bf16),
            dma((5,)),
            dma((groups, 2)), dma((groups, 2)),
            dma((groups,)), dma((groups,)),
            dma((1,)), dma((1,)),
            dma((1,)), dma((1,)),
            dma((groups, 3)), dma((groups, 3)),
            dma((groups, 3)), dma((groups, 3)),
            dma((groups, 3)), dma((groups, 3)),
            dma((groups, 3)), dma((groups, 3)),
            dma((groups, 3)), dma((groups, 3)),
            dma((groups, 3)), dma((groups, 3)),
        ],
        compiler_params=pltpu.CompilerParams(
            collective_id=0, has_side_effects=True, vmem_limit_bytes=VMEM_BYTES
        ),
    )(lengths, timestep_ids, guide_scale, here, hidden, weight)


def gathered(n, seqs, qkv, hidden, weight, lengths, timestep_ids, guide_scale):
    sample = lax.axis_index("dp")
    branch = lax.axis_index("branch")
    cols = weight.shape[1]
    length = lengths[sample]
    guidance = guide_scale[timestep_ids[sample]]
    here = lax.dynamic_slice_in_dim(qkv[0], branch * (seqs * cols), seqs * cols, axis=2)
    mine = lax.all_to_all(here, "seq", split_axis=2, concat_axis=0, tiled=True)
    tokens = mine.shape[0]
    heads = mine.reshape(tokens, 3, cols // HEAD_DIM, HEAD_DIM)
    queries, keys_all, values = heads[:, 0], heads[:, 1], heads[:, 2]
    scores = jnp.einsum(
        "qhd,khd->hqk", queries, keys_all, preferred_element_type=jnp.float32
    ) / math.sqrt(HEAD_DIM)
    positions = jnp.arange(tokens, dtype=jnp.int32)
    scores = jnp.where((positions < length)[None, None, :], scores, -jnp.inf)
    expo = jnp.exp(scores - jnp.max(scores, axis=-1, keepdims=True))
    probs = (expo / jnp.sum(expo, axis=-1, keepdims=True)).astype(jnp.bfloat16)
    strong = jnp.einsum("hqk,khd->qhd", probs, values, preferred_element_type=jnp.float32)
    strong = strong.astype(jnp.bfloat16).reshape(tokens, cols).astype(jnp.float32)
    weak = mine[:, 2, :].astype(jnp.float32)
    target = strong + guidance * (strong - weak)
    full = lax.all_gather(weight, "dp", axis=0, tiled=True)
    predicted = jnp.dot(hidden[0], full, preferred_element_type=jnp.float32)
    valid = (positions < length)[:, None]
    delta = (jnp.where(valid, predicted - target, jnp.float32(0.0)) / n).astype(jnp.bfloat16)
    deltas = lax.all_gather(delta, "dp", axis=0, tiled=True)
    slices = lax.all_to_all(hidden[0], "dp", split_axis=1, concat_axis=0, tiled=True)
    return lax.dot_general(
        slices, deltas, (((0,), (0,)), ((), ())), preferred_element_type=jnp.float32
    )


def solution(mesh):
    n, seqs = mesh.shape["dp"], mesh.shape["seq"]

    def local(qkv, hidden, weight, *rest):
        part, tokens = qkv.shape[1], hidden.shape[1]
        rows, cols = weight.shape
        need = 2 * (
            tokens * cols * (3 + 2 + 2 + 2 * n + 1) + tokens * rows * 3 * n // 2 + 4 * rows * cols
        )
        fits = (
            n == 8 and seqs == 2 and rows % 128 == 0 and cols % 256 == 0
            and part % 16 == 0 and tokens >= 96 and need < VMEM_BYTES * 3 // 4
        )
        return (fused if fits else gathered)(n, seqs, qkv, hidden, weight, *rest)

    in_specs = (
        P("dp", "seq", None, None),
        P("dp", None, None),
        P("dp", ("branch", "seq")),
        P(),
        P(),
        P(),
    )
    out_specs = P("dp", ("branch", "seq"))
    return jax.shard_map(local, mesh=mesh, in_specs=in_specs, out_specs=out_specs, check_vma=False)
```

```python
import functools
import math

import jax
import jax.numpy as jnp
from jax import lax
from jax.experimental import pallas as pl
from jax.experimental.pallas import tpu as pltpu
from jax.sharding import PartitionSpec as P

HEAD_DIM = 128
MESH = pl.DeviceIdType.MESH
VMEM_BYTES = 58500000


def flip(index, bits, count):
    out, step = 0, 1
    while step < count:
        bit = lax.rem(index // step, 2)
        out = out + (lax.rem(bit + 1, 2) if bits & step else bit) * step
        step *= 2
    return out


def splits(tokens):
    share = tokens // 2 // 16 * 16
    first = share * 3 // 7 // 16 * 16
    last = 16
    return share, (first, share - first), (first, share - first - last, last), 1

def kernel(
    n, seqs,
    lengths_ref, steps_ref, guide_ref, qkv_ref, hidden_ref, weight_ref, out_ref,
    len_s, step_s, guide_s,
    qbuf, hbuf, hx, wbuf, tgt, pf, pbuf, pown, prec, rbuf, dbuf, dsib,
    loc, one_r, one_s, h_r, f_r, p_r, g_r, d_r, r_r, x_r,
):
    groups = n // 2
    me = lax.axis_index("dp")
    branch, seq = lax.axis_index("branch"), lax.axis_index("seq")
    core = lax.rem(me, 2)
    group = me // 2
    sib = {"dp": group * 2 + (1 - core)}
    pair = {"seq": 1 - seq}
    part = qkv_ref.shape[1]
    tokens = hidden_ref.shape[1]
    rows, cols = weight_ref.shape
    other_groups = [flip(group, r, groups) for r in range(groups)]
    peers = [{"dp": g * 2 + core} for g in other_groups]
    share, a_sizes, b_sizes, n_straight = splits(tokens)
    direct = tokens - 2 * share
    early = share + direct

    regions = [(0, share, seq * share), (share, direct, 2 * share), (early, share, (1 - seq) * share)]
    regions = [(at, count, token) for at, count, token in regions if count]
    chunks = []
    for at, token, sizes in (
        (0, seq * share, a_sizes),
        (share, 2 * share, (direct,) if direct else ()),
        (early, (1 - seq) * share, b_sizes),
    ):
        for size in sizes:
            chunks.append((at, size, pl.multiple_of(token, 16)))
            at, token = at + size, token + size
    near_chunks = [c for c, chunk in enumerate(chunks) if chunk[0] < early]
    z_chunks = [c for c, chunk in enumerate(chunks) if chunk[0] >= early]
    straight = set(range(len(chunks) - n_straight, len(chunks)))
    tree = sum(chunk[1] for c, chunk in enumerate(chunks) if c not in straight)
    order = list(range(groups - 1, 0, -1))
    W, Q, E, H, Z, F, G, PT, PS, DT, DS, R, X = range(13)

    def send(kind, src, dst, recv, where):
        pltpu.make_async_remote_copy(
            src_ref=src, dst_ref=dst, send_sem=one_s.at[kind], recv_sem=recv,
            device_id=where, device_id_type=MESH,
        ).start()

    def take(ref, sem):
        pltpu.make_async_copy(ref, ref, sem).wait()

    def hid(g, region, start, width):
        base = pl.multiple_of(g * (2 * rows) + start, 128)
        return hidden_ref.at[0, pl.ds(pl.multiple_of(region[2], 16), region[1]), pl.ds(base, width)]

    def heads_of(to):
        return qkv_ref.at[:, :, pl.ds(pl.multiple_of((branch * seqs + to) * cols, 128), cols)]

    def at_rows(chunk):
        return pl.ds(chunk[0], chunk[1])

    barrier = pltpu.get_barrier_semaphore()
    for where in peers[1:] + [sib, pair]:
        pl.semaphore_signal(barrier, inc=1, device_id=where, device_id_type=MESH)
    my_rows = pl.ds(pl.multiple_of(core * rows, 128), rows)
    my_part = pl.ds(pl.multiple_of(seq * part, 16), part)
    other_rows = pl.ds(pl.multiple_of((1 - core) * rows, 128), rows)
    other_part = pl.ds(pl.multiple_of((1 - seq) * part, 16), part)
    for region in regions:
        pltpu.make_async_copy(hid(group, region, 0, 2 * rows), hbuf.at[0, at_rows(region)], loc.at[0]).start()
    pltpu.make_async_copy(weight_ref, wbuf.at[my_rows], loc.at[1]).start()
    pltpu.make_async_copy(heads_of(seq), qbuf.at[:, my_part], loc.at[2]).start()
    scalars = [
        pltpu.make_async_copy(ref, to, loc.at[3 + i])
        for i, (ref, to) in enumerate(((lengths_ref, len_s), (steps_ref, step_s), (guide_ref, guide_s)))
    ]
    for copy in scalars:
        copy.start()
    pl.semaphore_wait(barrier, groups + 1)

    for c in near_chunks:
        for r in order:
            send(H, hid(other_groups[r], chunks[c], 0, 2 * rows), hbuf.at[r, at_rows(chunks[c])], h_r.at[c], peers[r])
        if c == 0:
            send(Q, heads_of(1 - seq), qbuf.at[:, my_part], one_r.at[Q], pair)
            send(W, weight_ref, wbuf.at[my_rows], one_r.at[W], sib)
    for region in regions:
        send(E, hid(group, region, (1 - core) * rows, rows), hx.at[0, at_rows(region)], one_r.at[E], sib)

    halves = [None, slice(0, cols // 2), slice(cols // 2, cols)]

    def own():
        take(hbuf.at[0], loc.at[0])
        take(wbuf.at[my_rows], loc.at[1])
        take(wbuf.at[other_rows], one_r.at[W])
        pown[...] = jnp.dot(hbuf[0], wbuf[...], preferred_element_type=jnp.float32)

    def arrive(c):
        at, count, _ = chunks[c]
        take(hbuf.at[1:, at_rows(chunks[c])], h_r.at[c])
        if at < share:
            for to in z_chunks:
                start = chunks[to][0] - early
                if at <= start < at + count:
                    send(Z, hbuf.at[1:, pl.ds(start, chunks[to][1])], hbuf.at[1:, at_rows(chunks[to])], h_r.at[to], pair)
        send(F, hbuf.at[1:, at_rows(chunks[c]), other_rows], hx.at[1:, at_rows(chunks[c])], f_r.at[c], sib)

    def send_term(r, c, at):
        send(
            PS if c in straight else PT, pbuf.at[r, at_rows(chunks[c]), at],
            prec.at[r - 1, at_rows(chunks[c]), at], p_r.at[c], peers[r],
        )

    def predict(c):
        first, count, _ = chunks[c]
        left = hbuf[1:, first:first + count, :].reshape((groups - 1) * count, 2 * rows)
        value = jnp.dot(left, wbuf[...], preferred_element_type=jnp.float32).reshape(groups - 1, count, cols)
        if c in straight:
            for r in order:
                pbuf[r, first:first + count, :] = value[r - 1].astype(jnp.bfloat16)
                send_term(r, c, slice(0, cols))
            return
        for r in (1, 2):
            pbuf[3, first:first + count, halves[r]] = value[2, :, halves[r]].astype(jnp.bfloat16)
            send(
                G, pbuf.at[3, at_rows(chunks[c]), halves[r]], rbuf.at[r - 1, at_rows(chunks[c])],
                g_r.at[c], peers[r],
            )
        for r in (1, 2):
            pbuf[r, first:first + count, halves[r]] = value[r - 1, :, halves[r]].astype(jnp.bfloat16)
            send_term(r, c, halves[r])
        for r in (1, 2):
            pf[r - 1, first:first + count, :] = value[r - 1, :, halves[3 - r]]

    def combine(c):
        first, count, _ = chunks[c]
        take(rbuf.at[:, at_rows(chunks[c])], g_r.at[c])
        for r in (1, 2):
            to, at = 3 - r, halves[r]
            value = pf[to - 1, first:first + count, :] + rbuf[r - 1, first:first + count, :].astype(jnp.float32)
            pbuf[to, first:first + count, at] = value.astype(jnp.bfloat16)
            send_term(to, c, at)

    def to_sib(slots, c):
        send(X, dbuf.at[slots, at_rows(chunks[c])], dsib.at[slots, at_rows(chunks[c])], x_r.at[c], sib)

    def difference(c):
        first, count, token = chunks[c]
        near = 3 if c in straight else 2
        take(prec.at[0:near, at_rows(chunks[c])], p_r.at[c])
        total = pown[first:first + count, :] - tgt[pl.ds(token, count), :]
        for r in range(near):
            total = total + prec[r, first:first + count, :].astype(jnp.float32)
        length = len_s[me]
        valid = token + lax.broadcasted_iota(jnp.int32, total.shape, 0) < length
        delta = jnp.where(valid, total, jnp.float32(0.0)) * jnp.float32(1.0 / n)
        dbuf[0, first:first + count, :] = delta.astype(jnp.bfloat16)
        for r in order if c in straight else (1, 2):
            send(
                DS if c in straight else DT, dbuf.at[0, at_rows(chunks[c])], dbuf.at[r, at_rows(chunks[c])],
                d_r.at[c], peers[r],
            )
        to_sib(slice(0, 1), c)

    def relay(c):
        if c in straight:
            take(dbuf.at[1:, at_rows(chunks[c])], d_r.at[c])
            to_sib(slice(1, groups), c)
            return
        take(dbuf.at[1:3, at_rows(chunks[c])], d_r.at[c])
        for r in (1, 2):
            at = pl.ds((r - 1) * (cols // 2), cols // 2)
            send(
                R, dbuf.at[r, at_rows(chunks[c]), at], dbuf.at[3, at_rows(chunks[c]), at], r_r.at[c], peers[3 - r],
            )
        to_sib(slice(1, 3), c)

    def finish(c):
        take(dbuf.at[3, at_rows(chunks[c])], r_r.at[c])
        to_sib(slice(3, groups), c)

    def attend(first, last):
        if first == 0:
            for copy in scalars:
                copy.wait()
            take(qbuf.at[:, my_part], loc.at[2])
            take(qbuf.at[:, other_part], one_r.at[Q])
        length = len_s[me]
        guidance = guide_s[step_s[me]]
        key_valid = lax.broadcasted_iota(jnp.int32, (tokens, tokens), 1) < length

        @pl.loop(first, last)
        def _(h):
            at = pl.ds(pl.multiple_of(h * HEAD_DIM, HEAD_DIM), HEAD_DIM)
            q, k, v = qbuf[0, :, at], qbuf[1, :, at], qbuf[2, :, at]
            scores = lax.dot_general(
                q, k, (((1,), (1,)), ((), ())), preferred_element_type=jnp.float32
            ) * jnp.float32(1.0 / math.sqrt(HEAD_DIM))
            scores = jnp.where(key_valid, scores, -jnp.inf)
            maximum = jnp.max(scores, axis=-1, keepdims=True)
            expo = jnp.exp(scores - maximum)
            probs = (expo / jnp.sum(expo, axis=-1, keepdims=True)).astype(jnp.bfloat16)
            strong = jnp.dot(probs, v, preferred_element_type=jnp.float32)
            strong = strong.astype(jnp.bfloat16).astype(jnp.float32)
            tgt[:, at] = strong + guidance * (strong - v.astype(jnp.float32))

    def term(h_ref, base, d_ref, first, count):
        left = h_ref[:, first:first + count, pl.ds(base, rows)].reshape(groups * count, rows)
        right = d_ref[:, first:first + count, :].reshape(groups * count, cols)
        return lax.dot_general(left, right, (((0,), (0,)), ((), ())), preferred_element_type=jnp.float32)

    base = pl.multiple_of(core * rows, 128)

    def add_own(those, fresh=False):
        first = chunks[those[0]][0]
        count = sum(chunks[c][1] for c in those)
        value = term(hbuf, base, dbuf, first, count)
        out_ref[...] = value if fresh else out_ref[...] + value

    def add_sib(those, fresh=False):
        first = chunks[those[0]][0]
        count = sum(chunks[c][1] for c in those)
        if fresh:
            take(hx.at[0], one_r.at[E])
        for c in those:
            take(hx.at[1:, at_rows(chunks[c])], f_r.at[c])
            take(dsib.at[:, at_rows(chunks[c])], x_r.at[c])
        out_ref[...] += term(hx, 0, dsib, first, count)

    def add(those, fresh=False):
        add_own(those, fresh)
        add_sib(those, fresh)

    heads = cols // HEAD_DIM
    thirds = [0, heads // 3, 2 * heads // 3, heads]
    parts = [(thirds[i], thirds[i + 1]) for i in range(3)]
    own()
    arrive(0)
    predict(0)
    arrive(1)
    predict(1)
    attend(*parts[0])
    combine(0)
    attend(*parts[1])
    combine(1)
    attend(*parts[2])
    difference(0)
    difference(1)
    arrive(2)
    predict(2)
    relay(0)
    relay(1)
    combine(2)
    finish(0)
    finish(1)
    difference(2)
    arrive(3)
    predict(3)
    add((0, 1), True)
    combine(3)
    relay(2)
    difference(3)
    arrive(4)
    predict(4)
    finish(2)
    relay(3)
    difference(4)
    add((2,))
    finish(3)
    relay(4)
    add((3, 4))
    take(weight_ref, one_s.at[W])
    take(qbuf.at[:, my_part], one_s.at[Q])
    take(hx.at[0], one_s.at[E])
    take(hbuf.at[1:, pl.ds(0, early)], one_s.at[H])
    take(hbuf.at[1:, pl.ds(early, share)], one_s.at[Z])
    take(hx.at[1:], one_s.at[F])
    take(dsib, one_s.at[X])
    if tree:
        take(rbuf.at[:, pl.ds(0, tree)], one_s.at[G])
        take(prec.at[0:2, pl.ds(0, tree)], one_s.at[PT])
        take(dbuf.at[1:3, pl.ds(0, tree)], one_s.at[DT])
        take(dbuf.at[3, pl.ds(0, tree)], one_s.at[R])
    if tree < tokens:
        take(prec.at[:, pl.ds(tree, tokens - tree)], one_s.at[PS])
        take(dbuf.at[1:, pl.ds(tree, tokens - tree)], one_s.at[DS])


def fused(n, seqs, qkv, hidden, weight, lengths, timestep_ids, guide_scale):
    tokens = hidden.shape[1]
    rows, cols = weight.shape
    groups = n // 2
    share, a_sizes, b_sizes, _ = splits(tokens)
    count = len(a_sizes) + len(b_sizes) + (tokens > 2 * share)
    here = jnp.transpose(qkv[0], (1, 0, 2))
    dma = pltpu.SemaphoreType.DMA
    bf16, f32 = jnp.bfloat16, jnp.float32
    anywhere = pl.BlockSpec(memory_space=pltpu.HBM)
    return pl.pallas_call(
        functools.partial(kernel, n, seqs),
        out_shape=pltpu.VMEM((rows, cols), f32),
        in_specs=[anywhere] * 6,
        out_specs=pl.BlockSpec(memory_space=pltpu.VMEM),
        scratch_shapes=[
            pltpu.SMEM(lengths.shape, jnp.int32),
            pltpu.SMEM(timestep_ids.shape, jnp.int32),
            pltpu.SMEM(guide_scale.shape, f32),
            pltpu.VMEM((3, tokens, cols), bf16),
            pltpu.VMEM((groups, tokens, 2 * rows), bf16),
            pltpu.VMEM((groups, tokens, rows), bf16),
            pltpu.VMEM((2 * rows, cols), bf16),
            pltpu.VMEM((tokens, cols), f32),
            pltpu.VMEM((2, tokens, cols // 2), f32),
            pltpu.VMEM((groups, tokens, cols), bf16),
            pltpu.VMEM((tokens, cols), f32),
            pltpu.VMEM((groups - 1, tokens, cols), bf16),
            pltpu.VMEM((2, tokens, cols // 2), bf16),
            pltpu.VMEM((groups, tokens, cols), bf16),
            pltpu.VMEM((groups, tokens, cols), bf16),
            dma((6,)), dma((3,)), dma((13,)),
            *[dma((count,))] * 7,
        ],
        compiler_params=pltpu.CompilerParams(
            collective_id=0, has_side_effects=True, vmem_limit_bytes=VMEM_BYTES
        ),
    )(lengths, timestep_ids, guide_scale, here, hidden, weight)


def gathered(n, seqs, qkv, hidden, weight, lengths, timestep_ids, guide_scale):
    sample = lax.axis_index("dp")
    branch = lax.axis_index("branch")
    cols = weight.shape[1]
    length = lengths[sample]
    guidance = guide_scale[timestep_ids[sample]]
    here = lax.dynamic_slice_in_dim(qkv[0], branch * (seqs * cols), seqs * cols, axis=2)
    mine = lax.all_to_all(here, "seq", split_axis=2, concat_axis=0, tiled=True)
    tokens = mine.shape[0]
    heads = mine.reshape(tokens, 3, cols // HEAD_DIM, HEAD_DIM)
    queries, keys_all, values = heads[:, 0], heads[:, 1], heads[:, 2]
    scores = jnp.einsum(
        "qhd,khd->hqk", queries, keys_all, preferred_element_type=jnp.float32
    ) / math.sqrt(HEAD_DIM)
    positions = jnp.arange(tokens, dtype=jnp.int32)
    scores = jnp.where((positions < length)[None, None, :], scores, -jnp.inf)
    expo = jnp.exp(scores - jnp.max(scores, axis=-1, keepdims=True))
    probs = (expo / jnp.sum(expo, axis=-1, keepdims=True)).astype(jnp.bfloat16)
    strong = jnp.einsum("hqk,khd->qhd", probs, values, preferred_element_type=jnp.float32)
    strong = strong.astype(jnp.bfloat16).reshape(tokens, cols).astype(jnp.float32)
    weak = mine[:, 2, :].astype(jnp.float32)
    target = strong + guidance * (strong - weak)
    full = lax.all_gather(weight, "dp", axis=0, tiled=True)
    predicted = jnp.dot(hidden[0], full, preferred_element_type=jnp.float32)
    valid = (positions < length)[:, None]
    delta = (jnp.where(valid, predicted - target, jnp.float32(0.0)) / n).astype(jnp.bfloat16)
    deltas = lax.all_gather(delta, "dp", axis=0, tiled=True)
    slices = lax.all_to_all(hidden[0], "dp", split_axis=1, concat_axis=0, tiled=True)
    return lax.dot_general(
        slices, deltas, (((0,), (0,)), ((), ())), preferred_element_type=jnp.float32
    )


def solution(mesh):
    n, seqs = mesh.shape["dp"], mesh.shape["seq"]

    def local(qkv, hidden, weight, *rest):
        part, tokens = qkv.shape[1], hidden.shape[1]
        rows, cols = weight.shape
        need = 2 * (
            tokens * cols * (3 + 2 + 2 + 2 * n + 1) + tokens * rows * 3 * n // 2 + 4 * rows * cols
        )
        fits = (
            n == 8 and seqs == 2 and rows % 128 == 0 and cols % 256 == 0
            and part % 16 == 0 and tokens >= 96 and need < VMEM_BYTES * 3 // 4
        )
        return (fused if fits else gathered)(n, seqs, qkv, hidden, weight, *rest)

    in_specs = (
        P("dp", "seq", None, None),
        P("dp", None, None),
        P("dp", ("branch", "seq")),
        P(),
        P(),
        P(),
    )
    out_specs = P("dp", ("branch", "seq"))
    return jax.shard_map(local, mesh=mesh, in_specs=in_specs, out_specs=out_specs, check_vma=False)
```

```python
import functools
import math

import jax
import jax.numpy as jnp
from jax import lax
from jax.experimental import pallas as pl
from jax.experimental.pallas import tpu as pltpu
from jax.sharding import PartitionSpec as P

HEAD_DIM = 128
MESH = pl.DeviceIdType.MESH
VMEM_BYTES = 58500000


def flip(index, bits, count):
    out, step = 0, 1
    while step < count:
        bit = lax.rem(index // step, 2)
        out = out + (lax.rem(bit + 1, 2) if bits & step else bit) * step
        step *= 2
    return out


def splits(tokens):
    share = tokens * 3 // 7 // 16 * 16
    third = share // 3 // 16 * 16
    return share, (third, share - third), (third, third, share - 2 * third), 1

def kernel(
    n, seqs,
    lengths_ref, steps_ref, guide_ref, qkv_ref, hidden_ref, weight_ref, out_ref,
    len_s, step_s, guide_s,
    qbuf, hbuf, hx, wbuf, tgt, pf, pbuf, pown, prec, rbuf, dbuf, dsib,
    loc, one_r, one_s, h_r, f_r, p_r, g_r, d_r, r_r, x_r,
):
    groups = n // 2
    me = lax.axis_index("dp")
    branch, seq = lax.axis_index("branch"), lax.axis_index("seq")
    core = lax.rem(me, 2)
    group = me // 2
    sib = {"dp": group * 2 + (1 - core)}
    pair = {"seq": 1 - seq}
    part = qkv_ref.shape[1]
    tokens = hidden_ref.shape[1]
    rows, cols = weight_ref.shape
    other_groups = [flip(group, r, groups) for r in range(groups)]
    peers = [{"dp": g * 2 + core} for g in other_groups]
    share, a_sizes, b_sizes, n_straight = splits(tokens)
    direct = tokens - 2 * share
    early = share + direct

    regions = [(0, share, seq * share), (share, direct, 2 * share), (early, share, (1 - seq) * share)]
    regions = [(at, count, token) for at, count, token in regions if count]
    chunks = []
    for at, token, sizes in (
        (0, seq * share, a_sizes),
        (share, 2 * share, (direct,) if direct else ()),
        (early, (1 - seq) * share, b_sizes),
    ):
        for size in sizes:
            chunks.append((at, size, pl.multiple_of(token, 16)))
            at, token = at + size, token + size
    near_chunks = [c for c, chunk in enumerate(chunks) if chunk[0] < early]
    z_chunks = [c for c, chunk in enumerate(chunks) if chunk[0] >= early]
    straight = set(range(len(chunks) - n_straight, len(chunks)))
    tree = sum(chunk[1] for c, chunk in enumerate(chunks) if c not in straight)
    order = list(range(groups - 1, 0, -1))
    W, Q, E, H, Z, F, G, PT, PS, DT, DS, R, X = range(13)

    def send(kind, src, dst, recv, where):
        pltpu.make_async_remote_copy(
            src_ref=src, dst_ref=dst, send_sem=one_s.at[kind], recv_sem=recv,
            device_id=where, device_id_type=MESH,
        ).start()

    def take(ref, sem):
        pltpu.make_async_copy(ref, ref, sem).wait()

    def hid(g, region, start, width):
        base = pl.multiple_of(g * (2 * rows) + start, 128)
        return hidden_ref.at[0, pl.ds(pl.multiple_of(region[2], 16), region[1]), pl.ds(base, width)]

    def heads_of(to):
        return qkv_ref.at[:, :, pl.ds(pl.multiple_of((branch * seqs + to) * cols, 128), cols)]

    def at_rows(chunk):
        return pl.ds(chunk[0], chunk[1])

    barrier = pltpu.get_barrier_semaphore()
    for where in peers[1:] + [sib, pair]:
        pl.semaphore_signal(barrier, inc=1, device_id=where, device_id_type=MESH)
    my_rows = pl.ds(pl.multiple_of(core * rows, 128), rows)
    my_part = pl.ds(pl.multiple_of(seq * part, 16), part)
    other_rows = pl.ds(pl.multiple_of((1 - core) * rows, 128), rows)
    other_part = pl.ds(pl.multiple_of((1 - seq) * part, 16), part)
    for region in regions:
        pltpu.make_async_copy(hid(group, region, 0, 2 * rows), hbuf.at[0, at_rows(region)], loc.at[0]).start()
    pltpu.make_async_copy(weight_ref, wbuf.at[my_rows], loc.at[1]).start()
    pltpu.make_async_copy(heads_of(seq), qbuf.at[:, my_part], loc.at[2]).start()
    scalars = [
        pltpu.make_async_copy(ref, to, loc.at[3 + i])
        for i, (ref, to) in enumerate(((lengths_ref, len_s), (steps_ref, step_s), (guide_ref, guide_s)))
    ]
    for copy in scalars:
        copy.start()
    pl.semaphore_wait(barrier, groups + 1)

    for c in near_chunks:
        for r in order:
            send(H, hid(other_groups[r], chunks[c], 0, 2 * rows), hbuf.at[r, at_rows(chunks[c])], h_r.at[c], peers[r])
        if c == 0:
            send(Q, heads_of(1 - seq), qbuf.at[:, my_part], one_r.at[Q], pair)
            send(W, weight_ref, wbuf.at[my_rows], one_r.at[W], sib)
    for region in regions:
        send(E, hid(group, region, (1 - core) * rows, rows), hx.at[0, at_rows(region)], one_r.at[E], sib)

    halves = [None, slice(0, cols // 2), slice(cols // 2, cols)]

    def own():
        take(hbuf.at[0], loc.at[0])
        take(wbuf.at[my_rows], loc.at[1])
        take(wbuf.at[other_rows], one_r.at[W])
        pown[...] = jnp.dot(hbuf[0], wbuf[...], preferred_element_type=jnp.float32)

    def arrive(c):
        at, count, _ = chunks[c]
        take(hbuf.at[1:, at_rows(chunks[c])], h_r.at[c])
        if at < share:
            for to in z_chunks:
                start = chunks[to][0] - early
                if at <= start < at + count:
                    send(Z, hbuf.at[1:, pl.ds(start, chunks[to][1])], hbuf.at[1:, at_rows(chunks[to])], h_r.at[to], pair)
        send(F, hbuf.at[1:, at_rows(chunks[c]), other_rows], hx.at[1:, at_rows(chunks[c])], f_r.at[c], sib)

    def send_term(r, c, at):
        send(
            PS if c in straight else PT, pbuf.at[r, at_rows(chunks[c]), at],
            prec.at[r - 1, at_rows(chunks[c]), at], p_r.at[c], peers[r],
        )

    def predict(c):
        first, count, _ = chunks[c]
        left = hbuf[1:, first:first + count, :].reshape((groups - 1) * count, 2 * rows)
        value = jnp.dot(left, wbuf[...], preferred_element_type=jnp.float32).reshape(groups - 1, count, cols)
        if c in straight:
            for r in order:
                pbuf[r, first:first + count, :] = value[r - 1].astype(jnp.bfloat16)
                send_term(r, c, slice(0, cols))
            return
        for r in (1, 2):
            pbuf[3, first:first + count, halves[r]] = value[2, :, halves[r]].astype(jnp.bfloat16)
            send(
                G, pbuf.at[3, at_rows(chunks[c]), halves[r]], rbuf.at[r - 1, at_rows(chunks[c])],
                g_r.at[c], peers[r],
            )
        for r in (1, 2):
            pbuf[r, first:first + count, halves[r]] = value[r - 1, :, halves[r]].astype(jnp.bfloat16)
            send_term(r, c, halves[r])
        for r in (1, 2):
            pf[r - 1, first:first + count, :] = value[r - 1, :, halves[3 - r]]

    def combine(c):
        first, count, _ = chunks[c]
        take(rbuf.at[:, at_rows(chunks[c])], g_r.at[c])
        for r in (1, 2):
            to, at = 3 - r, halves[r]
            value = pf[to - 1, first:first + count, :] + rbuf[r - 1, first:first + count, :].astype(jnp.float32)
            pbuf[to, first:first + count, at] = value.astype(jnp.bfloat16)
            send_term(to, c, at)

    def to_sib(slots, c):
        send(X, dbuf.at[slots, at_rows(chunks[c])], dsib.at[slots, at_rows(chunks[c])], x_r.at[c], sib)

    def difference(c):
        first, count, token = chunks[c]
        near = 3 if c in straight else 2
        take(prec.at[0:near, at_rows(chunks[c])], p_r.at[c])
        total = pown[first:first + count, :] - tgt[pl.ds(token, count), :]
        for r in range(near):
            total = total + prec[r, first:first + count, :].astype(jnp.float32)
        length = len_s[me]
        valid = token + lax.broadcasted_iota(jnp.int32, total.shape, 0) < length
        delta = jnp.where(valid, total, jnp.float32(0.0)) * jnp.float32(1.0 / n)
        dbuf[0, first:first + count, :] = delta.astype(jnp.bfloat16)
        for r in order if c in straight else (1, 2):
            send(
                DS if c in straight else DT, dbuf.at[0, at_rows(chunks[c])], dbuf.at[r, at_rows(chunks[c])],
                d_r.at[c], peers[r],
            )
        to_sib(slice(0, 1), c)

    def relay(c):
        if c in straight:
            take(dbuf.at[1:, at_rows(chunks[c])], d_r.at[c])
            to_sib(slice(1, groups), c)
            return
        take(dbuf.at[1:3, at_rows(chunks[c])], d_r.at[c])
        for r in (1, 2):
            at = pl.ds((r - 1) * (cols // 2), cols // 2)
            send(
                R, dbuf.at[r, at_rows(chunks[c]), at], dbuf.at[3, at_rows(chunks[c]), at], r_r.at[c], peers[3 - r],
            )
        to_sib(slice(1, 3), c)

    def finish(c):
        take(dbuf.at[3, at_rows(chunks[c])], r_r.at[c])
        to_sib(slice(3, groups), c)

    def attend(first, last):
        if first == 0:
            for copy in scalars:
                copy.wait()
            take(qbuf.at[:, my_part], loc.at[2])
            take(qbuf.at[:, other_part], one_r.at[Q])
        length = len_s[me]
        guidance = guide_s[step_s[me]]
        key_valid = lax.broadcasted_iota(jnp.int32, (tokens, tokens), 1) < length

        @pl.loop(first, last)
        def _(h):
            at = pl.ds(pl.multiple_of(h * HEAD_DIM, HEAD_DIM), HEAD_DIM)
            q, k, v = qbuf[0, :, at], qbuf[1, :, at], qbuf[2, :, at]
            scores = lax.dot_general(
                q, k, (((1,), (1,)), ((), ())), preferred_element_type=jnp.float32
            ) * jnp.float32(1.0 / math.sqrt(HEAD_DIM))
            scores = jnp.where(key_valid, scores, -jnp.inf)
            maximum = jnp.max(scores, axis=-1, keepdims=True)
            expo = jnp.exp(scores - maximum)
            probs = (expo / jnp.sum(expo, axis=-1, keepdims=True)).astype(jnp.bfloat16)
            strong = jnp.dot(probs, v, preferred_element_type=jnp.float32)
            strong = strong.astype(jnp.bfloat16).astype(jnp.float32)
            tgt[:, at] = strong + guidance * (strong - v.astype(jnp.float32))

    def term(h_ref, base, d_ref, first, count):
        left = h_ref[:, first:first + count, pl.ds(base, rows)].reshape(groups * count, rows)
        right = d_ref[:, first:first + count, :].reshape(groups * count, cols)
        return lax.dot_general(left, right, (((0,), (0,)), ((), ())), preferred_element_type=jnp.float32)

    base = pl.multiple_of(core * rows, 128)

    def add_own(those, fresh=False):
        first = chunks[those[0]][0]
        count = sum(chunks[c][1] for c in those)
        value = term(hbuf, base, dbuf, first, count)
        out_ref[...] = value if fresh else out_ref[...] + value

    def add_sib(those, fresh=False):
        first = chunks[those[0]][0]
        count = sum(chunks[c][1] for c in those)
        if fresh:
            take(hx.at[0], one_r.at[E])
        for c in those:
            take(hx.at[1:, at_rows(chunks[c])], f_r.at[c])
            take(dsib.at[:, at_rows(chunks[c])], x_r.at[c])
        out_ref[...] += term(hx, 0, dsib, first, count)

    def add(those, fresh=False):
        add_own(those, fresh)
        add_sib(those, fresh)

    heads = cols // HEAD_DIM
    thirds = [0, heads // 3, 2 * heads // 3, heads]
    parts = [(thirds[i], thirds[i + 1]) for i in range(3)]
    own()
    arrive(0)
    predict(0)
    arrive(1)
    predict(1)
    attend(*parts[0])
    combine(0)
    arrive(2)
    predict(2)
    attend(*parts[1])
    arrive(3)
    combine(1)
    predict(3)
    attend(*parts[2])
    combine(2)
    difference(0)
    difference(1)
    arrive(4)
    combine(3)
    predict(4)
    difference(2)
    difference(3)
    combine(4)
    relay(0)
    arrive(5)
    relay(2)
    predict(5)
    relay(3)
    difference(4)
    relay(1)
    difference(5)
    relay(4)
    finish(2)
    finish(0)
    finish(3)
    finish(1)
    add((3,), True)
    add((0,1,2,))
    relay(5)
    finish(4)
    add((4,5,))
    take(weight_ref, one_s.at[W])
    take(qbuf.at[:, my_part], one_s.at[Q])
    take(hx.at[0], one_s.at[E])
    take(hbuf.at[1:, pl.ds(0, early)], one_s.at[H])
    take(hbuf.at[1:, pl.ds(early, share)], one_s.at[Z])
    take(hx.at[1:], one_s.at[F])
    take(dsib, one_s.at[X])
    if tree:
        take(rbuf.at[:, pl.ds(0, tree)], one_s.at[G])
        take(prec.at[0:2, pl.ds(0, tree)], one_s.at[PT])
        take(dbuf.at[1:3, pl.ds(0, tree)], one_s.at[DT])
        take(dbuf.at[3, pl.ds(0, tree)], one_s.at[R])
    if tree < tokens:
        take(prec.at[:, pl.ds(tree, tokens - tree)], one_s.at[PS])
        take(dbuf.at[1:, pl.ds(tree, tokens - tree)], one_s.at[DS])


def fused(n, seqs, qkv, hidden, weight, lengths, timestep_ids, guide_scale):
    tokens = hidden.shape[1]
    rows, cols = weight.shape
    groups = n // 2
    share, a_sizes, b_sizes, _ = splits(tokens)
    count = len(a_sizes) + len(b_sizes) + (tokens > 2 * share)
    here = jnp.transpose(qkv[0], (1, 0, 2))
    dma = pltpu.SemaphoreType.DMA
    bf16, f32 = jnp.bfloat16, jnp.float32
    anywhere = pl.BlockSpec(memory_space=pltpu.HBM)
    return pl.pallas_call(
        functools.partial(kernel, n, seqs),
        out_shape=pltpu.VMEM((rows, cols), f32),
        in_specs=[anywhere] * 6,
        out_specs=pl.BlockSpec(memory_space=pltpu.VMEM),
        scratch_shapes=[
            pltpu.SMEM(lengths.shape, jnp.int32),
            pltpu.SMEM(timestep_ids.shape, jnp.int32),
            pltpu.SMEM(guide_scale.shape, f32),
            pltpu.VMEM((3, tokens, cols), bf16),
            pltpu.VMEM((groups, tokens, 2 * rows), bf16),
            pltpu.VMEM((groups, tokens, rows), bf16),
            pltpu.VMEM((2 * rows, cols), bf16),
            pltpu.VMEM((tokens, cols), f32),
            pltpu.VMEM((2, tokens, cols // 2), f32),
            pltpu.VMEM((groups, tokens, cols), bf16),
            pltpu.VMEM((tokens, cols), f32),
            pltpu.VMEM((groups - 1, tokens, cols), bf16),
            pltpu.VMEM((2, tokens, cols // 2), bf16),
            pltpu.VMEM((groups, tokens, cols), bf16),
            pltpu.VMEM((groups, tokens, cols), bf16),
            dma((6,)), dma((3,)), dma((13,)),
            *[dma((count,))] * 7,
        ],
        compiler_params=pltpu.CompilerParams(
            collective_id=0, has_side_effects=True, vmem_limit_bytes=VMEM_BYTES
        ),
    )(lengths, timestep_ids, guide_scale, here, hidden, weight)


def gathered(n, seqs, qkv, hidden, weight, lengths, timestep_ids, guide_scale):
    sample = lax.axis_index("dp")
    branch = lax.axis_index("branch")
    cols = weight.shape[1]
    length = lengths[sample]
    guidance = guide_scale[timestep_ids[sample]]
    here = lax.dynamic_slice_in_dim(qkv[0], branch * (seqs * cols), seqs * cols, axis=2)
    mine = lax.all_to_all(here, "seq", split_axis=2, concat_axis=0, tiled=True)
    tokens = mine.shape[0]
    heads = mine.reshape(tokens, 3, cols // HEAD_DIM, HEAD_DIM)
    queries, keys_all, values = heads[:, 0], heads[:, 1], heads[:, 2]
    scores = jnp.einsum(
        "qhd,khd->hqk", queries, keys_all, preferred_element_type=jnp.float32
    ) / math.sqrt(HEAD_DIM)
    positions = jnp.arange(tokens, dtype=jnp.int32)
    scores = jnp.where((positions < length)[None, None, :], scores, -jnp.inf)
    expo = jnp.exp(scores - jnp.max(scores, axis=-1, keepdims=True))
    probs = (expo / jnp.sum(expo, axis=-1, keepdims=True)).astype(jnp.bfloat16)
    strong = jnp.einsum("hqk,khd->qhd", probs, values, preferred_element_type=jnp.float32)
    strong = strong.astype(jnp.bfloat16).reshape(tokens, cols).astype(jnp.float32)
    weak = mine[:, 2, :].astype(jnp.float32)
    target = strong + guidance * (strong - weak)
    full = lax.all_gather(weight, "dp", axis=0, tiled=True)
    predicted = jnp.dot(hidden[0], full, preferred_element_type=jnp.float32)
    valid = (positions < length)[:, None]
    delta = (jnp.where(valid, predicted - target, jnp.float32(0.0)) / n).astype(jnp.bfloat16)
    deltas = lax.all_gather(delta, "dp", axis=0, tiled=True)
    slices = lax.all_to_all(hidden[0], "dp", split_axis=1, concat_axis=0, tiled=True)
    return lax.dot_general(
        slices, deltas, (((0,), (0,)), ((), ())), preferred_element_type=jnp.float32
    )


def solution(mesh):
    n, seqs = mesh.shape["dp"], mesh.shape["seq"]

    def local(qkv, hidden, weight, *rest):
        part, tokens = qkv.shape[1], hidden.shape[1]
        rows, cols = weight.shape
        need = 2 * (
            tokens * cols * (3 + 2 + 2 + 2 * n + 1) + tokens * rows * 3 * n // 2 + 4 * rows * cols
        )
        fits = (
            n == 8 and seqs == 2 and rows % 128 == 0 and cols % 256 == 0
            and part % 16 == 0 and tokens % 16 == 0 and tokens >= 128 and need < VMEM_BYTES * 3 // 4
        )
        return (fused if fits else gathered)(n, seqs, qkv, hidden, weight, *rest)

    in_specs = (
        P("dp", "seq", None, None),
        P("dp", None, None),
        P("dp", ("branch", "seq")),
        P(),
        P(),
        P(),
    )
    out_specs = P("dp", ("branch", "seq"))
    return jax.shard_map(local, mesh=mesh, in_specs=in_specs, out_specs=out_specs, check_vma=False)
```

```python
import functools
import math

import jax
import jax.numpy as jnp
from jax import lax
from jax.experimental import pallas as pl
from jax.experimental.pallas import tpu as pltpu
from jax.sharding import PartitionSpec as P

HEAD_DIM = 128
MESH = pl.DeviceIdType.MESH
VMEM_BYTES = 58500000


def flip(index, bits, count):
    out, step = 0, 1
    while step < count:
        bit = lax.rem(index // step, 2)
        out = out + (lax.rem(bit + 1, 2) if bits & step else bit) * step
        step *= 2
    return out


def splits(tokens):
    share = tokens * 3 // 7 // 16 * 16
    third = share // 3 // 16 * 16
    return share, (third, share - third), (third, third, share - 2 * third), 1

def kernel(
    n, seqs,
    lengths_ref, steps_ref, guide_ref, qkv_ref, hidden_ref, weight_ref, out_ref,
    len_s, step_s, guide_s,
    qbuf, hbuf, hx, wbuf, tgt, pf, pbuf, pown, prec, rbuf, dbuf, dsib,
    met, loc, one_r, one_s, h_r, p_r, g_r, d_r, r_r, x_r,
):
    groups = n // 2
    me = lax.axis_index("dp")
    branch, seq = lax.axis_index("branch"), lax.axis_index("seq")
    core = lax.rem(me, 2)
    group = me // 2
    sib = {"dp": group * 2 + (1 - core)}
    pair = {"seq": 1 - seq}
    part = qkv_ref.shape[1]
    tokens = hidden_ref.shape[1]
    rows, cols = weight_ref.shape
    other_groups = [flip(group, r, groups) for r in range(groups)]
    peers = [{"dp": g * 2 + core} for g in other_groups]
    share, a_sizes, b_sizes, n_straight = splits(tokens)
    direct = tokens - 2 * share
    early = share + direct

    regions = [(0, share, seq * share), (share, direct, 2 * share), (early, share, (1 - seq) * share)]
    regions = [(at, count, token) for at, count, token in regions if count]
    chunks = []
    for at, token, sizes in (
        (0, seq * share, a_sizes),
        (share, 2 * share, (direct,) if direct else ()),
        (early, (1 - seq) * share, b_sizes),
    ):
        for size in sizes:
            chunks.append((at, size, pl.multiple_of(token, 16)))
            at, token = at + size, token + size
    near_chunks = [c for c, chunk in enumerate(chunks) if chunk[0] < early]
    z_chunks = [c for c, chunk in enumerate(chunks) if chunk[0] >= early]
    straight = set(range(len(chunks) - n_straight, len(chunks)))
    tree = sum(chunk[1] for c, chunk in enumerate(chunks) if c not in straight)
    order = list(range(groups - 1, 0, -1))
    W, Q, E, F, H, G, PT, PS, DS, X = range(10)

    def send(kind, src, dst, recv, where):
        pltpu.make_async_remote_copy(
            src_ref=src, dst_ref=dst, send_sem=one_s.at[kind], recv_sem=recv,
            device_id=where, device_id_type=MESH,
        ).start()

    def take(ref, sem):
        pltpu.make_async_copy(ref, ref, sem).wait()

    def hid(g, region, start, width):
        base = pl.multiple_of(g * (2 * rows) + start, 128)
        return hidden_ref.at[0, pl.ds(pl.multiple_of(region[2], 16), region[1]), pl.ds(base, width)]

    def heads_of(to):
        return qkv_ref.at[:, :, pl.ds(pl.multiple_of((branch * seqs + to) * cols, 128), cols)]

    def at_rows(chunk):
        return pl.ds(chunk[0], chunk[1])

    barrier = pltpu.get_barrier_semaphore()
    near = peers[1:3] + [sib, pair]
    for where in near:
        pl.semaphore_signal(barrier, inc=1, device_id=where, device_id_type=MESH)
    my_rows = pl.ds(pl.multiple_of(core * rows, 128), rows)
    my_part = pl.ds(pl.multiple_of(seq * part, 16), part)
    other_rows = pl.ds(pl.multiple_of((1 - core) * rows, 128), rows)
    other_part = pl.ds(pl.multiple_of((1 - seq) * part, 16), part)
    for region in regions:
        pltpu.make_async_copy(hid(group, region, 0, 2 * rows), hbuf.at[0, at_rows(region)], loc.at[0]).start()
    pltpu.make_async_copy(weight_ref, wbuf.at[my_rows], loc.at[1]).start()
    pltpu.make_async_copy(heads_of(seq), qbuf.at[:, my_part], loc.at[2]).start()
    scalars = [
        pltpu.make_async_copy(ref, to, loc.at[3 + i])
        for i, (ref, to) in enumerate(((lengths_ref, len_s), (steps_ref, step_s), (guide_ref, guide_s)))
    ]
    for copy in scalars:
        copy.start()
    pl.semaphore_wait(barrier, len(near))
    pl.semaphore_signal(met, inc=1, device_id=peers[1], device_id_type=MESH)

    for c in near_chunks:
        for r in (2, 1, 3):
            if (c, r) == (0, 3):
                send(Q, heads_of(1 - seq), qbuf.at[:, my_part], one_r.at[Q], pair)
                send(W, weight_ref, wbuf.at[my_rows], one_r.at[W], sib)
                pl.semaphore_wait(met, 1)
            send(H, hid(other_groups[r], chunks[c], 0, 2 * rows), hbuf.at[r, at_rows(chunks[c])], h_r.at[c], peers[r])
    for region in regions:
        send(E, hid(group, region, (1 - core) * rows, rows), hx.at[0, at_rows(region)], one_r.at[E], sib)

    halves = [None, slice(0, cols // 2), slice(cols // 2, cols)]

    def own():
        take(hbuf.at[0], loc.at[0])
        take(wbuf.at[my_rows], loc.at[1])
        take(wbuf.at[other_rows], one_r.at[W])
        pown[...] = jnp.dot(hbuf[0], wbuf[...], preferred_element_type=jnp.float32)

    def arrive(c):
        at, count, _ = chunks[c]
        take(hbuf.at[1:, at_rows(chunks[c])], h_r.at[c])
        if at < share:
            for to in z_chunks:
                start = chunks[to][0] - early
                if at <= start < at + count:
                    send(H, hbuf.at[1:, pl.ds(start, chunks[to][1])], hbuf.at[1:, at_rows(chunks[to])], h_r.at[to], pair)
        send(F, hbuf.at[1:, at_rows(chunks[c]), other_rows], hx.at[1:, at_rows(chunks[c])], one_r.at[F], sib)

    def send_term(r, c, at):
        send(
            PS if c in straight else PT, pbuf.at[r, at_rows(chunks[c]), at],
            prec.at[r - 1, at_rows(chunks[c]), at], p_r.at[c], peers[r],
        )

    def predict(c):
        first, count, _ = chunks[c]
        left = hbuf[1:, first:first + count, :].reshape((groups - 1) * count, 2 * rows)
        value = jnp.dot(left, wbuf[...], preferred_element_type=jnp.float32).reshape(groups - 1, count, cols)
        if c in straight:
            for r in (2, 1, 3):
                pbuf[r, first:first + count, :] = value[r - 1].astype(jnp.bfloat16)
                send_term(r, c, slice(0, cols))
            return
        for r in (1, 2):
            pbuf[3, first:first + count, halves[r]] = value[2, :, halves[r]].astype(jnp.bfloat16)
            send(
                G, pbuf.at[3, at_rows(chunks[c]), halves[r]], rbuf.at[r - 1, at_rows(chunks[c])],
                g_r.at[c], peers[r],
            )
        for r in (1, 2):
            pbuf[r, first:first + count, halves[r]] = value[r - 1, :, halves[r]].astype(jnp.bfloat16)
            send_term(r, c, halves[r])
        for r in (1, 2):
            pf[r - 1, first:first + count, :] = value[r - 1, :, halves[3 - r]]

    def combine(c):
        first, count, _ = chunks[c]
        take(rbuf.at[:, at_rows(chunks[c])], g_r.at[c])
        for r in (1, 2):
            to, at = 3 - r, halves[r]
            value = pf[to - 1, first:first + count, :] + rbuf[r - 1, first:first + count, :].astype(jnp.float32)
            pbuf[to, first:first + count, at] = value.astype(jnp.bfloat16)
            send_term(to, c, at)

    def to_sib(slots, c):
        send(X, dbuf.at[slots, at_rows(chunks[c])], dsib.at[slots, at_rows(chunks[c])], x_r.at[c], sib)

    def difference(c):
        first, count, token = chunks[c]
        near = 3 if c in straight else 2
        take(prec.at[0:near, at_rows(chunks[c])], p_r.at[c])
        total = pown[first:first + count, :] - tgt[pl.ds(token, count), :]
        for r in range(near):
            total = total + prec[r, first:first + count, :].astype(jnp.float32)
        length = len_s[me]
        valid = token + lax.broadcasted_iota(jnp.int32, total.shape, 0) < length
        delta = jnp.where(valid, total, jnp.float32(0.0)) * jnp.float32(1.0 / n)
        dbuf[0, first:first + count, :] = delta.astype(jnp.bfloat16)
        for r in (2, 1, 3) if c in straight else (1, 2):
            send(
                DS if c in straight else PT, dbuf.at[0, at_rows(chunks[c])], dbuf.at[r, at_rows(chunks[c])],
                d_r.at[c], peers[r],
            )
        to_sib(slice(0, 1), c)

    def relay(c):
        if c in straight:
            take(dbuf.at[1:, at_rows(chunks[c])], d_r.at[c])
            to_sib(slice(1, groups), c)
            return
        take(dbuf.at[1:3, at_rows(chunks[c])], d_r.at[c])
        for r in (1, 2):
            at = pl.ds((r - 1) * (cols // 2), cols // 2)
            send(
                G, dbuf.at[r, at_rows(chunks[c]), at], dbuf.at[3, at_rows(chunks[c]), at], r_r.at[c], peers[3 - r],
            )
        to_sib(slice(1, 3), c)

    def finish(c):
        take(dbuf.at[3, at_rows(chunks[c])], r_r.at[c])
        to_sib(slice(3, groups), c)

    def attend(first, last):
        if first == 0:
            for copy in scalars:
                copy.wait()
            take(qbuf.at[:, my_part], loc.at[2])
            take(qbuf.at[:, other_part], one_r.at[Q])
        length = len_s[me]
        guidance = guide_s[step_s[me]]
        key_valid = lax.broadcasted_iota(jnp.int32, (tokens, tokens), 1) < length

        @pl.loop(first, last)
        def _(h):
            at = pl.ds(pl.multiple_of(h * HEAD_DIM, HEAD_DIM), HEAD_DIM)
            q, k, v = qbuf[0, :, at], qbuf[1, :, at], qbuf[2, :, at]
            scores = lax.dot_general(
                q, k, (((1,), (1,)), ((), ())), preferred_element_type=jnp.float32
            ) * jnp.float32(1.0 / math.sqrt(HEAD_DIM))
            scores = jnp.where(key_valid, scores, -jnp.inf)
            maximum = jnp.max(scores, axis=-1, keepdims=True)
            expo = jnp.exp(scores - maximum)
            probs = (expo / jnp.sum(expo, axis=-1, keepdims=True)).astype(jnp.bfloat16)
            strong = jnp.dot(probs, v, preferred_element_type=jnp.float32)
            strong = strong.astype(jnp.bfloat16).astype(jnp.float32)
            tgt[:, at] = strong + guidance * (strong - v.astype(jnp.float32))

    def term(h_ref, base, d_ref, first, count):
        left = h_ref[:, first:first + count, pl.ds(base, rows)].reshape(groups * count, rows)
        right = d_ref[:, first:first + count, :].reshape(groups * count, cols)
        return lax.dot_general(left, right, (((0,), (0,)), ((), ())), preferred_element_type=jnp.float32)

    base = pl.multiple_of(core * rows, 128)

    def add_own(those, fresh=False):
        first = chunks[those[0]][0]
        count = sum(chunks[c][1] for c in those)
        value = term(hbuf, base, dbuf, first, count)
        out_ref[...] = value if fresh else out_ref[...] + value

    def add_sib(those, fresh=False):
        first = chunks[those[0]][0]
        count = sum(chunks[c][1] for c in those)
        if fresh:
            take(hx.at[0], one_r.at[E])
            take(hx.at[1:], one_r.at[F])
        for c in those:
            take(dsib.at[:, at_rows(chunks[c])], x_r.at[c])
        out_ref[...] += term(hx, 0, dsib, first, count)

    def add(those, fresh=False):
        add_own(those, fresh)
        add_sib(those, fresh)

    heads = cols // HEAD_DIM
    thirds = [0, heads // 3, 2 * heads // 3, heads]
    parts = [(thirds[i], thirds[i + 1]) for i in range(3)]
    own()
    arrive(0)
    predict(0)
    arrive(1)
    predict(1)
    attend(*parts[0])
    combine(0)
    arrive(2)
    predict(2)
    attend(*parts[1])
    arrive(3)
    combine(1)
    predict(3)
    attend(*parts[2])
    combine(2)
    difference(0)
    difference(1)
    arrive(4)
    combine(3)
    predict(4)
    difference(2)
    relay(0)
    difference(3)
    combine(4)
    arrive(5)
    relay(2)
    predict(5)
    relay(3)
    difference(4)
    relay(1)
    difference(5)
    relay(4)
    finish(2)
    finish(0)
    finish(3)
    finish(1)
    add((3,), True)
    add((0,1,2,))
    relay(5)
    finish(4)
    add((4,5,))
    take(weight_ref, one_s.at[W])
    take(qbuf.at[:, my_part], one_s.at[Q])
    take(hx.at[0], one_s.at[E])
    take(hbuf.at[1:], one_s.at[H])
    take(hx.at[1:], one_s.at[F])
    take(dsib, one_s.at[X])
    if tree:
        take(prec.at[0:2, pl.ds(0, tree)], one_s.at[G])
        take(dbuf.at[:, pl.ds(0, tree)], one_s.at[PT])
    if tree < tokens:
        take(prec.at[:, pl.ds(tree, tokens - tree)], one_s.at[PS])
        take(dbuf.at[1:, pl.ds(tree, tokens - tree)], one_s.at[DS])


def fused(n, seqs, qkv, hidden, weight, lengths, timestep_ids, guide_scale):
    tokens = hidden.shape[1]
    rows, cols = weight.shape
    groups = n // 2
    share, a_sizes, b_sizes, _ = splits(tokens)
    count = len(a_sizes) + len(b_sizes) + (tokens > 2 * share)
    here = jnp.transpose(qkv[0], (1, 0, 2))
    dma = pltpu.SemaphoreType.DMA
    bf16, f32 = jnp.bfloat16, jnp.float32
    anywhere = pl.BlockSpec(memory_space=pltpu.HBM)
    return pl.pallas_call(
        functools.partial(kernel, n, seqs),
        out_shape=pltpu.VMEM((rows, cols), f32),
        in_specs=[anywhere] * 6,
        out_specs=pl.BlockSpec(memory_space=pltpu.VMEM),
        scratch_shapes=[
            pltpu.SMEM(lengths.shape, jnp.int32),
            pltpu.SMEM(timestep_ids.shape, jnp.int32),
            pltpu.SMEM(guide_scale.shape, f32),
            pltpu.VMEM((3, tokens, cols), bf16),
            pltpu.VMEM((groups, tokens, 2 * rows), bf16),
            pltpu.VMEM((groups, tokens, rows), bf16),
            pltpu.VMEM((2 * rows, cols), bf16),
            pltpu.VMEM((tokens, cols), f32),
            pltpu.VMEM((2, tokens, cols // 2), f32),
            pltpu.VMEM((groups, tokens, cols), bf16),
            pltpu.VMEM((tokens, cols), f32),
            pltpu.VMEM((groups - 1, tokens, cols), bf16),
            pltpu.VMEM((2, tokens, cols // 2), bf16),
            pltpu.VMEM((groups, tokens, cols), bf16),
            pltpu.VMEM((groups, tokens, cols), bf16),
            pltpu.SemaphoreType.REGULAR, dma((6,)), dma((4,)), dma((10,)),
            *[dma((count,))] * 6,
        ],
        compiler_params=pltpu.CompilerParams(
            collective_id=0, has_side_effects=True, vmem_limit_bytes=VMEM_BYTES
        ),
    )(lengths, timestep_ids, guide_scale, here, hidden, weight)


def gathered(n, seqs, qkv, hidden, weight, lengths, timestep_ids, guide_scale):
    sample = lax.axis_index("dp")
    branch = lax.axis_index("branch")
    cols = weight.shape[1]
    length = lengths[sample]
    guidance = guide_scale[timestep_ids[sample]]
    here = lax.dynamic_slice_in_dim(qkv[0], branch * (seqs * cols), seqs * cols, axis=2)
    mine = lax.all_to_all(here, "seq", split_axis=2, concat_axis=0, tiled=True)
    tokens = mine.shape[0]
    heads = mine.reshape(tokens, 3, cols // HEAD_DIM, HEAD_DIM)
    queries, keys_all, values = heads[:, 0], heads[:, 1], heads[:, 2]
    scores = jnp.einsum(
        "qhd,khd->hqk", queries, keys_all, preferred_element_type=jnp.float32
    ) / math.sqrt(HEAD_DIM)
    positions = jnp.arange(tokens, dtype=jnp.int32)
    scores = jnp.where((positions < length)[None, None, :], scores, -jnp.inf)
    expo = jnp.exp(scores - jnp.max(scores, axis=-1, keepdims=True))
    probs = (expo / jnp.sum(expo, axis=-1, keepdims=True)).astype(jnp.bfloat16)
    strong = jnp.einsum("hqk,khd->qhd", probs, values, preferred_element_type=jnp.float32)
    strong = strong.astype(jnp.bfloat16).reshape(tokens, cols).astype(jnp.float32)
    weak = mine[:, 2, :].astype(jnp.float32)
    target = strong + guidance * (strong - weak)
    full = lax.all_gather(weight, "dp", axis=0, tiled=True)
    predicted = jnp.dot(hidden[0], full, preferred_element_type=jnp.float32)
    valid = (positions < length)[:, None]
    delta = (jnp.where(valid, predicted - target, jnp.float32(0.0)) / n).astype(jnp.bfloat16)
    deltas = lax.all_gather(delta, "dp", axis=0, tiled=True)
    slices = lax.all_to_all(hidden[0], "dp", split_axis=1, concat_axis=0, tiled=True)
    return lax.dot_general(
        slices, deltas, (((0,), (0,)), ((), ())), preferred_element_type=jnp.float32
    )


def solution(mesh):
    n, seqs = mesh.shape["dp"], mesh.shape["seq"]

    def local(qkv, hidden, weight, *rest):
        part, tokens = qkv.shape[1], hidden.shape[1]
        rows, cols = weight.shape
        need = 2 * (
            tokens * cols * (3 + 2 + 2 + 2 * n + 1) + tokens * rows * 3 * n // 2 + 4 * rows * cols
        )
        fits = (
            n == 8 and seqs == 2 and rows % 128 == 0 and cols % 256 == 0
            and part % 16 == 0 and tokens % 16 == 0 and tokens >= 128 and need < VMEM_BYTES * 3 // 4
        )
        return (fused if fits else gathered)(n, seqs, qkv, hidden, weight, *rest)

    in_specs = (
        P("dp", "seq", None, None),
        P("dp", None, None),
        P("dp", ("branch", "seq")),
        P(),
        P(),
        P(),
    )
    out_specs = P("dp", ("branch", "seq"))
    return jax.shard_map(local, mesh=mesh, in_specs=in_specs, out_specs=out_specs, check_vma=False)
```
